128 devices in a mesh: section: 2 (over z_hi), dp: 8 (over z_lo, x), expert: 8 (over y, core).
Axes of the slice: x: 4, y: 4, z: 4 (z_hi: 2, z_lo: 2; z = z_hi * 2 + z_lo), core: 2. Of those that a mesh axis runs over, the one named last changes fastest.
Arguments:
- tokens: bfloat16 [2, 16384, 3584], P('section', ('dp', 'expert')), may hold values from -0.75 to 0.75
- routes: int32 [2, 16384, 2], P('section', ('dp', 'expert')), may hold values from 0 to 7, all different within a row; in each aligned block of 256 rows (0 to 255, 256 to 511, ..., all dimensions but the last counted through in order) at most 80 rows name the same one
- hidden_grad: bfloat16 [2, 8, 8, 640, 1024], P('section', 'dp', 'expert'), may hold values from -1.5 to 1.5
- w_gate: bfloat16 [2, 8, 3584, 1024], P('section', 'expert'), may hold values from -0.75 to 0.75
- w_up: bfloat16 [2, 8, 3584, 1024], P('section', 'expert'), may hold values from -0.75 to 0.75
Outputs:
- passed_grad: bfloat16 [2, 16384, 3584], P('section', ('dp', 'expert'))
- grad_gate: bfloat16 [2, 8, 3584, 1024], P('section', 'expert', 'dp')
- grad_up: bfloat16 [2, 8, 3584, 1024], P('section', 'expert', 'dp')
The draws below stay inside these ranges and needn't reach their ends.
Inputs may be any that keep to these rules, and one draw needn't show every extreme that they name: `routes`: each token names 2 different experts. Among the 256 tokens of one device at most 80 name the same expert, and in every draw some device's tokens name some expert exactly 80 times.
All inputs are finite; a program needn't handle non-finite values.
Results may differ from the reference program's by a relative error of at most 0.019.
Values may be sent and summed in bfloat16 or wider, within the bound.
A program may use at most 192 MiB of HBM per device.

```python
import math
import jax
import jax.numpy as jnp
import numpy as np

D = 3584
FF = 1024
TOP = 2
TOK_DEV = 256
EXPERTS = 8
CAP = 80
SLOTS = 640
TOKENS = 16384
N_SECTION = 2
N_DP = 8
N_EXPERT = 8


def steps_of(rng, extent, cuts, least, largest):
    gain, own = 1.0, jax.random.fold_in(rng, 6)
    for position, shards_of in cuts:
        steps = jnp.exp(jax.random.uniform(jax.random.fold_in(own, position), (shards_of,), jnp.float32, least / len(cuts), largest / len(cuts)))
        gain = gain * jnp.repeat(steps, extent[position] // shards_of).reshape([-1 if axis == position else 1 for axis in range(len(extent))])
    return gain


def deal_out(own_key, own, number, rows, number_of, top, most, slope):
    sequence = jax.random.permutation(own_key, number_of)
    heavy_load, usual = load_shares(number_of, rows * top, most, slope, True), load_shares(number_of, rows * top, most, slope, False)
    places = jnp.arange(number_of)

    def named(lengths, offset_by):
        used = int((lengths > 0).sum())
        fixed = max(1, used // 4)
        shifted = fixed + (places - fixed + offset_by * (used - fixed)) % max(1, number_of - fixed)
        return jnp.zeros((number_of,), jnp.int32).at[sequence[jnp.where(places < fixed, places, shifted)]].set(jnp.asarray(lengths, jnp.int32))

    lengths = jnp.where(number % 4 == 0, named(heavy_load, number // 4), named(usual, number - number // 4 - 1))
    mixed = jax.random.permutation(jax.random.fold_in(own, 3), number_of)
    giver, taker = mixed[0:number_of // 2 * 2:2], mixed[1:number_of // 2 * 2:2]
    room = jnp.minimum(lengths[giver] - 1, most - lengths[taker]) // 2
    room = jnp.where((giver == sequence[0]) | (taker == sequence[0]) | (lengths[taker] == 0), 0, jnp.maximum(room, 0))
    shifted = jax.random.randint(jax.random.fold_in(own, 4), (number_of // 2,), 0, 1 << 20) % (room + 1)
    lengths = lengths.at[giver].add(-shifted).at[taker].add(shifted)
    labels = jnp.searchsorted(jnp.cumsum(lengths), jnp.arange(rows * top), side="right").astype(jnp.int32)
    grid = labels.reshape(top, rows).T
    grid = grid[jax.random.permutation(jax.random.fold_in(own, 1), rows)]
    offset_by = jax.random.randint(jax.random.fold_in(own, 2), (rows, 1), 0, top)
    return jnp.take_along_axis(grid, (jnp.arange(top)[None, :] + offset_by) % top, axis=1)


def load_shares(amount, total, limit, slope, full):
    portions = [(1 << 20) // math.isqrt(rank ** slope) + 1 for rank in range(1, amount + 1)]
    largest = limit if full else min(limit, max(-(-total // amount), total * portions[0] // sum(portions)))
    least = 1 if total - largest >= amount - 1 else 0
    holding, surplus = [largest] + [least] * (amount - 1), total - largest - least * (amount - 1)
    while surplus > 0:
        candidates = [i for i in range(1, amount) if holding[i] < largest] or [i for i in range(1, amount) if holding[i] < limit]
        pool, remaining = sum([portions[i] for i in candidates]), surplus
        for i in candidates:
            extra = min(limit - holding[i], max(1, remaining * portions[i] // pool), surplus)
            holding[i] = holding[i] + extra
            surplus = surplus - extra
    return np.array(holding)


def scatter_about(own_key, shape, deviation, most, pieces=(), kind=jnp.bfloat16):
    loudness = steps_of(own_key, shape, pieces, -0.22, 0.18) if pieces else 1.0
    result = jax.random.normal(own_key, shape, jnp.float32) * deviation * loudness
    return jnp.minimum(jnp.maximum(result, -most), most).astype(kind)


def setup_inputs(seed: int = 0) -> dict:
    arg_keys = jax.random.split(jax.random.key(seed), 6)
    tokens = scatter_about(arg_keys[0], (N_SECTION, TOKENS, D), 0.125, 0.75, ((0, 2), (1, 64)))
    routes_keys = jax.random.split(jax.random.fold_in(arg_keys[1], 1), N_SECTION * TOKENS // TOK_DEV)
    routes_turns = jax.random.permutation(jax.random.fold_in(arg_keys[1], 3), N_SECTION * TOKENS // TOK_DEV)
    routes = jax.vmap(lambda own, number: deal_out(jax.random.fold_in(arg_keys[1], 2), own, number, TOK_DEV, EXPERTS, TOP, CAP, 1))(routes_keys, routes_turns).reshape((N_SECTION, TOKENS, TOP))
    hidden_grad = scatter_about(arg_keys[2], (N_SECTION, N_DP, EXPERTS, SLOTS, FF), 0.25, 1.5, ((0, 2), (1, 8), (2, 8)))
    w_gate = scatter_about(arg_keys[3], (N_SECTION, EXPERTS, D, FF), (D // 64) ** -0.5, 0.75, ((0, 2), (1, 8)))
    w_up = scatter_about(arg_keys[4], (N_SECTION, EXPERTS, D, FF), (D // 64) ** -0.5, 0.75, ((0, 2), (1, 8)))
    return {"tokens": tokens, "routes": routes, "hidden_grad": hidden_grad, "w_gate": w_gate, "w_up": w_up}


def slot_numbers(route_rows, experts, capacity):
    marked = (route_rows[:, :, None] == jnp.arange(experts, dtype=jnp.int32)[None, None, :]).astype(jnp.int32)
    per_token = jnp.sum(marked, axis=1).astype(jnp.int32)
    earlier = (jnp.cumsum(per_token, axis=0) - per_token).astype(jnp.int32)
    within = jnp.sum(marked * earlier[:, None, :], axis=2).astype(jnp.int32)
    return (route_rows * capacity + within).astype(jnp.int32)


def sender_rows(token_rows, slots, slot_total):
    token_count = token_rows.shape[0]
    top_slots = slots.shape[1]
    owner = jnp.full((slot_total,), token_count, jnp.int32)
    owner = owner.at[slots.reshape(-1)].set(jnp.repeat(jnp.arange(token_count, dtype=jnp.int32), top_slots))
    padded = jnp.concatenate([token_rows, jnp.zeros((1, token_rows.shape[1]), token_rows.dtype)], axis=0)
    return padded[owner]


def swiglu_grads(grad_hidden, gate_pre, up_pre):
    sigmoid_gate = jax.nn.sigmoid(gate_pre)
    grad_gate_pre = grad_hidden * up_pre * sigmoid_gate * (1.0 + gate_pre * (1.0 - sigmoid_gate))
    grad_up_pre = grad_hidden * gate_pre * sigmoid_gate
    return grad_gate_pre.astype(jnp.bfloat16), grad_up_pre.astype(jnp.bfloat16)


def reference(tokens, routes, hidden_grad, w_gate, w_up):
    experts = EXPERTS
    capacity = CAP
    slot_total = SLOTS
    section_grads = []
    gate_out = []
    up_out = []
    for section_index in range(N_SECTION):
        gate_sums = [jnp.zeros((D, FF), jnp.float32) for expert_index in range(experts)]
        up_sums = [jnp.zeros((D, FF), jnp.float32) for expert_index in range(experts)]
        token_parts = []
        for group_index in range(N_DP):
            base = group_index * N_EXPERT * TOK_DEV
            slot_lists = []
            outgoing = []
            for source in range(N_EXPERT):
                first = base + source * TOK_DEV
                token_rows = tokens[section_index, first:first + TOK_DEV]
                slots = slot_numbers(routes[section_index, first:first + TOK_DEV], experts, capacity)
                slot_lists.append(slots)
                outgoing.append(sender_rows(token_rows, slots, slot_total).reshape(experts, capacity, D))
            returned_parts = []
            for expert_index in range(experts):
                received = jnp.concatenate([outgoing[source][expert_index] for source in range(N_EXPERT)], axis=0)
                gate_w = w_gate[section_index, expert_index]
                up_w = w_up[section_index, expert_index]
                gate_pre = jnp.dot(received, gate_w, preferred_element_type=jnp.float32)
                up_pre = jnp.dot(received, up_w, preferred_element_type=jnp.float32)
                grad_hidden = hidden_grad[section_index, group_index, expert_index].astype(jnp.float32)
                grad_gate_pre, grad_up_pre = swiglu_grads(grad_hidden, gate_pre, up_pre)
                slot_grad = (jnp.dot(grad_gate_pre, gate_w.T, preferred_element_type=jnp.float32)
                             + jnp.dot(grad_up_pre, up_w.T, preferred_element_type=jnp.float32)).astype(jnp.bfloat16)
                returned_parts.append(slot_grad.reshape(N_EXPERT, capacity, D))
                gate_sums[expert_index] = gate_sums[expert_index] + jnp.dot(received.T, grad_gate_pre, preferred_element_type=jnp.float32)
                up_sums[expert_index] = up_sums[expert_index] + jnp.dot(received.T, grad_up_pre, preferred_element_type=jnp.float32)
            for source in range(N_EXPERT):
                returned = jnp.concatenate([returned_parts[expert_index][source] for expert_index in range(experts)], axis=0)
                picked = returned[slot_lists[source]].astype(jnp.float32)
                token_parts.append(jnp.sum(picked, axis=1).astype(jnp.bfloat16))
        section_grads.append(jnp.concatenate(token_parts, axis=0))
        gate_out.append(jnp.stack([total.astype(jnp.bfloat16) for total in gate_sums], axis=0))
        up_out.append(jnp.stack([total.astype(jnp.bfloat16) for total in up_sums], axis=0))
    token_grad = jnp.stack(section_grads, axis=0)
    passed_grad = jnp.roll(token_grad, -1, axis=0)
    return passed_grad, jnp.stack(gate_out, axis=0), jnp.stack(up_out, axis=0)
```

```python
import jax
import jax.numpy as jnp
from jax import lax
from jax.sharding import PartitionSpec as P


def from_behind(value, axis, by):
    count = lax.axis_size(axis)
    return lax.ppermute(value, axis, [(i, (i + by) % count) for i in range(count)])


def slot_numbers(route_rows, experts, capacity):
    marked = (route_rows[:, :, None] == jnp.arange(experts, dtype=jnp.int32)[None, None, :]).astype(
        jnp.int32
    )
    per_token = jnp.sum(marked, axis=1)
    earlier = jnp.cumsum(per_token, axis=0) - per_token
    within = jnp.sum(marked * earlier[:, None, :], axis=2)
    return route_rows * capacity + within


def slot_owner(slots, slot_total):
    hit = slots[None, :, :] == jnp.arange(slot_total, dtype=jnp.int32)[:, None, None]
    return jnp.any(hit, axis=2).astype(jnp.bfloat16)


def swiglu_grads(grad_hidden, gate_pre, up_pre):
    sigmoid_gate = jax.nn.sigmoid(gate_pre)
    grad_gate_pre = grad_hidden * up_pre * sigmoid_gate * (1.0 + gate_pre * (1.0 - sigmoid_gate))
    grad_up_pre = grad_hidden * gate_pre * sigmoid_gate
    return (grad_gate_pre.astype(jnp.bfloat16), grad_up_pre.astype(jnp.bfloat16))


def shards(tokens, routes, hidden_grad, w_gate, w_up):
    experts = lax.axis_size("expert")
    slot_total = hidden_grad.shape[3]
    capacity = slot_total // experts
    width = tokens.shape[2]
    slots = slot_numbers(routes[0], experts, capacity)
    owner = slot_owner(slots, slot_total)
    outgoing = jnp.dot(owner, tokens[0], preferred_element_type=jnp.float32).astype(jnp.bfloat16)
    received = lax.all_to_all(
        outgoing.reshape(experts, capacity, width),
        "expert",
        split_axis=0,
        concat_axis=0,
        tiled=True,
    )
    received = received.reshape(slot_total, width)
    gate_w = w_gate[0, 0]
    up_w = w_up[0, 0]
    hidden = gate_w.shape[1]
    gate_pre = jnp.dot(received, gate_w, preferred_element_type=jnp.float32)
    up_pre = jnp.dot(received, up_w, preferred_element_type=jnp.float32)
    grad_gate_pre, grad_up_pre = swiglu_grads(
        hidden_grad[0, 0, 0].astype(jnp.float32), gate_pre, up_pre
    )
    both_grads = jnp.concatenate([grad_gate_pre, grad_up_pre], axis=1)
    along_slots = (((0,), (0,)), ((), ()))
    summed = lax.psum_scatter(
        lax.dot_general(
            received, both_grads, along_slots, preferred_element_type=jnp.float32
        ).astype(jnp.bfloat16),
        "dp",
        scatter_dimension=0,
        tiled=True,
    ).astype(jnp.float32)
    grad_gate = summed[:, :hidden].astype(jnp.bfloat16)[None, None]
    grad_up = summed[:, hidden:].astype(jnp.bfloat16)[None, None]

    gather_back = owner.T
    along_hidden = (((1,), (1,)), ((), ()))
    pieces = 4
    step = width // pieces
    passed = []
    for piece in range(pieces):
        cols = slice(piece * step, (piece + 1) * step)
        slot_grad = (
            lax.dot_general(grad_gate_pre, gate_w[cols], along_hidden, preferred_element_type=jnp.float32)
            + lax.dot_general(grad_up_pre, up_w[cols], along_hidden, preferred_element_type=jnp.float32)
        ).astype(jnp.bfloat16)
        returned = lax.all_to_all(
            slot_grad.reshape(experts, capacity, step),
            "expert",
            split_axis=0,
            concat_axis=0,
            tiled=True,
        ).reshape(slot_total, step)
        token_grad = jnp.dot(gather_back, returned, preferred_element_type=jnp.float32).astype(
            jnp.bfloat16
        )
        passed.append(from_behind(token_grad, "section", -1))
    passed_grad = jnp.concatenate(passed, axis=1)[None]
    return (passed_grad, grad_gate, grad_up)


def solution(mesh):
    placed = (
        P("section", ("dp", "expert"), None),
        P("section", ("dp", "expert"), None),
        P("section", "dp", "expert", None, None),
        P("section", "expert", None, None),
        P("section", "expert", None, None),
    )
    return jax.shard_map(
        shards,
        mesh=mesh,
        in_specs=placed,
        out_specs=(
            P("section", ("dp", "expert"), None),
            P("section", "expert", "dp", None),
            P("section", "expert", "dp", None),
        ),
        check_vma=False,
    )
```

```python
import jax
import jax.numpy as jnp
from jax import lax
from jax.sharding import PartitionSpec as P


def from_behind(value, axis, by):
    count = lax.axis_size(axis)
    return lax.ppermute(value, axis, [(i, (i + by) % count) for i in range(count)])


def across_sections(value, way):
    sections = lax.axis_size("section")
    groups = lax.axis_size("dp")
    lows = 2
    rows = groups // lows
    ring = sections * lows

    def place(z, x):
        return (z // lows) * groups + (z % lows) * rows + x

    perm = [
        (place(z, x), place((z + way) % ring, x)) for z in range(ring) for x in range(rows)
    ]
    hop = lax.ppermute(value, ("section", "dp"), perm)
    return lax.ppermute(hop, ("section", "dp"), perm)


def slot_numbers(route_rows, experts, capacity):
    marked = (route_rows[:, :, None] == jnp.arange(experts, dtype=jnp.int32)[None, None, :]).astype(
        jnp.int32
    )
    per_token = jnp.sum(marked, axis=1)
    earlier = jnp.cumsum(per_token, axis=0) - per_token
    within = jnp.sum(marked * earlier[:, None, :], axis=2)
    return route_rows * capacity + within


def slot_owner(slots, slot_total):
    hit = slots[None, :, :] == jnp.arange(slot_total, dtype=jnp.int32)[:, None, None]
    return jnp.any(hit, axis=2).astype(jnp.bfloat16)


def swiglu_grads(grad_hidden, gate_pre, up_pre):
    sigmoid_gate = jax.nn.sigmoid(gate_pre)
    grad_gate_pre = grad_hidden * up_pre * sigmoid_gate * (1.0 + gate_pre * (1.0 - sigmoid_gate))
    grad_up_pre = grad_hidden * gate_pre * sigmoid_gate
    return (grad_gate_pre.astype(jnp.bfloat16), grad_up_pre.astype(jnp.bfloat16))


def shards(tokens, routes, hidden_grad, w_gate, w_up):
    experts = lax.axis_size("expert")
    slot_total = hidden_grad.shape[3]
    capacity = slot_total // experts
    width = tokens.shape[2]
    slots = slot_numbers(routes[0], experts, capacity)
    owner = slot_owner(slots, slot_total)
    outgoing = jnp.dot(owner, tokens[0], preferred_element_type=jnp.float32).astype(jnp.bfloat16)
    received = lax.all_to_all(
        outgoing.reshape(experts, capacity, width),
        "expert",
        split_axis=0,
        concat_axis=0,
        tiled=True,
    )
    received = received.reshape(slot_total, width)
    gate_w = w_gate[0, 0]
    up_w = w_up[0, 0]
    hidden = gate_w.shape[1]
    gate_pre = jnp.dot(received, gate_w, preferred_element_type=jnp.float32)
    up_pre = jnp.dot(received, up_w, preferred_element_type=jnp.float32)
    grad_gate_pre, grad_up_pre = swiglu_grads(
        hidden_grad[0, 0, 0].astype(jnp.float32), gate_pre, up_pre
    )
    both_grads = jnp.concatenate([grad_gate_pre, grad_up_pre], axis=1)
    along_slots = (((0,), (0,)), ((), ()))
    summed = lax.psum_scatter(
        lax.dot_general(
            received, both_grads, along_slots, preferred_element_type=jnp.float32
        ).astype(jnp.bfloat16),
        "dp",
        scatter_dimension=0,
        tiled=True,
    ).astype(jnp.float32)
    grad_gate = summed[:, :hidden].astype(jnp.bfloat16)[None, None]
    grad_up = summed[:, hidden:].astype(jnp.bfloat16)[None, None]

    gather_back = owner.T
    along_hidden = (((1,), (1,)), ((), ()))
    pieces = 4
    step = width // pieces
    passed = []
    for piece in range(pieces):
        cols = slice(piece * step, (piece + 1) * step)
        slot_grad = (
            lax.dot_general(grad_gate_pre, gate_w[cols], along_hidden, preferred_element_type=jnp.float32)
            + lax.dot_general(grad_up_pre, up_w[cols], along_hidden, preferred_element_type=jnp.float32)
        ).astype(jnp.bfloat16)
        returned = lax.all_to_all(
            slot_grad.reshape(experts, capacity, step),
            "expert",
            split_axis=0,
            concat_axis=0,
            tiled=True,
        ).reshape(slot_total, step)
        token_grad = jnp.dot(gather_back, returned, preferred_element_type=jnp.float32).astype(
            jnp.bfloat16
        )
        passed.append(across_sections(token_grad, 1 if piece % 2 == 0 else -1))
    passed_grad = jnp.concatenate(passed, axis=1)[None]
    return (passed_grad, grad_gate, grad_up)


def solution(mesh):
    placed = (
        P("section", ("dp", "expert"), None),
        P("section", ("dp", "expert"), None),
        P("section", "dp", "expert", None, None),
        P("section", "expert", None, None),
        P("section", "expert", None, None),
    )
    return jax.shard_map(
        shards,
        mesh=mesh,
        in_specs=placed,
        out_specs=(
            P("section", ("dp", "expert"), None),
            P("section", "expert", "dp", None),
            P("section", "expert", "dp", None),
        ),
        check_vma=False,
    )
```

```python
import jax
import jax.numpy as jnp
from jax import lax
from jax.sharding import PartitionSpec as P


def from_behind(value, axis, by):
    count = lax.axis_size(axis)
    return lax.ppermute(value, axis, [(i, (i + by) % count) for i in range(count)])


def across_sections(value, way):
    sections = lax.axis_size("section")
    groups = lax.axis_size("dp")
    lows = 2
    rows = groups // lows
    ring = sections * lows

    def place(z, x):
        return (z // lows) * groups + (z % lows) * rows + x

    perm = [
        (place(z, x), place((z + way) % ring, x)) for z in range(ring) for x in range(rows)
    ]
    hop = lax.ppermute(value, ("section", "dp"), perm)
    return lax.ppermute(hop, ("section", "dp"), perm)


def slot_numbers(route_rows, experts, capacity):
    marked = (route_rows[:, :, None] == jnp.arange(experts, dtype=jnp.int32)[None, None, :]).astype(
        jnp.int32
    )
    per_token = jnp.sum(marked, axis=1)
    earlier = jnp.cumsum(per_token, axis=0) - per_token
    within = jnp.sum(marked * earlier[:, None, :], axis=2)
    return route_rows * capacity + within


def slot_owner(slots, slot_total):
    hit = slots[None, :, :] == jnp.arange(slot_total, dtype=jnp.int32)[:, None, None]
    return jnp.any(hit, axis=2).astype(jnp.bfloat16)


def swiglu_grads(grad_hidden, gate_pre, up_pre):
    sigmoid_gate = jax.nn.sigmoid(gate_pre)
    grad_gate_pre = grad_hidden * up_pre * sigmoid_gate * (1.0 + gate_pre * (1.0 - sigmoid_gate))
    grad_up_pre = grad_hidden * gate_pre * sigmoid_gate
    return (grad_gate_pre.astype(jnp.bfloat16), grad_up_pre.astype(jnp.bfloat16))


def shards(tokens, routes, hidden_grad, w_gate, w_up):
    experts = lax.axis_size("expert")
    slot_total = hidden_grad.shape[3]
    capacity = slot_total // experts
    width = tokens.shape[2]
    slots = slot_numbers(routes[0], experts, capacity)
    owner = slot_owner(slots, slot_total)
    outgoing = jnp.dot(owner, tokens[0], preferred_element_type=jnp.float32).astype(jnp.bfloat16)
    gate_w = w_gate[0, 0]
    up_w = w_up[0, 0]
    hidden = gate_w.shape[1]
    groups = lax.axis_size("dp")
    shard = width // groups
    parts = 4
    part = shard // parts

    def columns(value, j):
        lead = value.shape[:-1]
        return value.reshape(lead + (groups, parts, part))[..., j, :].reshape(lead + (groups * part,))

    received = []
    gate_pre = None
    up_pre = None
    for j in range(parts):
        cols = slice(j * (width // parts), (j + 1) * (width // parts))
        got = lax.all_to_all(
            outgoing[:, cols].reshape(experts, capacity, width // parts),
            "expert",
            split_axis=0,
            concat_axis=0,
            tiled=True,
        ).reshape(slot_total, width // parts)
        received.append(got)
        gate_part = jnp.dot(got, gate_w[cols], preferred_element_type=jnp.float32)
        up_part = jnp.dot(got, up_w[cols], preferred_element_type=jnp.float32)
        gate_pre = gate_part if gate_pre is None else gate_pre + gate_part
        up_pre = up_part if up_pre is None else up_pre + up_part
    grad_gate_pre, grad_up_pre = swiglu_grads(
        hidden_grad[0, 0, 0].astype(jnp.float32), gate_pre, up_pre
    )
    both_grads = jnp.concatenate([grad_gate_pre, grad_up_pre], axis=1)
    along_slots = (((0,), (0,)), ((), ()))
    received = jnp.concatenate(received, axis=1)
    summed = []
    for j in range(parts):
        summed.append(
            lax.psum_scatter(
                lax.dot_general(
                    columns(received, j), both_grads, along_slots, preferred_element_type=jnp.float32
                ).astype(jnp.bfloat16),
                "dp",
                scatter_dimension=0,
                tiled=True,
            )
        )
    summed = jnp.concatenate(summed, axis=0)
    grad_gate = summed[:, :hidden][None, None]
    grad_up = summed[:, hidden:][None, None]

    gather_back = owner.T
    along_hidden = (((1,), (1,)), ((), ()))
    pieces = 4
    step = width // pieces
    passed = []
    for piece in range(pieces):
        cols = slice(piece * step, (piece + 1) * step)
        slot_grad = (
            lax.dot_general(grad_gate_pre, gate_w[cols], along_hidden, preferred_element_type=jnp.float32)
            + lax.dot_general(grad_up_pre, up_w[cols], along_hidden, preferred_element_type=jnp.float32)
        ).astype(jnp.bfloat16)
        returned = lax.all_to_all(
            slot_grad.reshape(experts, capacity, step),
            "expert",
            split_axis=0,
            concat_axis=0,
            tiled=True,
        ).reshape(slot_total, step)
        token_grad = jnp.dot(gather_back, returned, preferred_element_type=jnp.float32).astype(
            jnp.bfloat16
        )
        passed.append(across_sections(token_grad, 1 if piece % 2 == 0 else -1))
    passed_grad = jnp.concatenate(passed, axis=1)[None]
    return (passed_grad, grad_gate, grad_up)


def solution(mesh):
    placed = (
        P("section", ("dp", "expert"), None),
        P("section", ("dp", "expert"), None),
        P("section", "dp", "expert", None, None),
        P("section", "expert", None, None),
        P("section", "expert", None, None),
    )
    return jax.shard_map(
        shards,
        mesh=mesh,
        in_specs=placed,
        out_specs=(
            P("section", ("dp", "expert"), None),
            P("section", "expert", "dp", None),
            P("section", "expert", "dp", None),
        ),
        check_vma=False,
    )
```
